32 devices in a mesh: grp: 4 (over y, x), sub: 8 (over z, core).
Axes of the slice: x: 2, y: 2, z: 4, core: 2. Of those that a mesh axis runs over, the one named last changes fastest.
Arguments:
- residual: bfloat16 [4, 8, 1024, 2048], P('grp', 'sub'), may hold values from -6 to 6
- inverse_blocks: bfloat16 [4, 8, 1024, 1536], P('grp', 'sub'), may hold values from -0.15625 to 0.15625
- operator_tiles: bfloat16 [4, 8, 8, 8, 128, 128], P('grp', 'sub'), may hold values from -0.1875 to 0.1875
- column_blocks: int32 [4, 8, 8, 8], P('grp', 'sub'), may hold values from 0 to 11
- coarse_basis: bfloat16 [4, 8, 1024, 200], P('grp', 'sub'), may hold values from -6 to 6
- face_rows: int32 [4, 8, 4, 128], P('grp', 'sub'), may hold values from 0 to 1023
Outputs:
- local_fix: bfloat16 [4, 8, 1024, 2048], P('grp', 'sub')
- galerkin: float32 [200, 200], replicated
- coarse_rhs: float32 [200, 2048], P(None, 'sub')
The draws below stay inside these ranges and needn't reach their ends.
All inputs are finite; a program needn't handle non-finite values.
Results may differ from the reference program's by a relative error of at most 0.0029.
Values may be sent and summed in bfloat16 or wider, within the bound.
A program may use at most 128 MiB of HBM per device.

```python
import math
import jax
import jax.numpy as jnp
from jax import lax

ROWS = 1024
OV = 128
K = 2048
C = 200
TILE = 128
NNZB = 8
EXT = 1536
RB = 8
EB = 12
N_GRP = 4
N_SUB = 8


def with_ends(result, stream_key, least, largest):
    shape = result.shape
    spot = [jax.random.randint(jax.random.fold_in(stream_key, axis), (), 0, shape[axis]) for axis in range(len(shape))]
    result = result.at[tuple(spot)].set(least)
    longest = shape.index(max(shape))
    spot[longest] = (spot[longest] + 1) % shape[longest]
    return result.at[tuple(spot)].set(largest)


def strengthened(values, key, source, target, blocks, factor):
    def block_of(dim):
        return (jnp.arange(values.shape[dim]) // (values.shape[dim] // blocks)).reshape((-1,) + (1,) * (values.ndim - 1 - dim))

    first = jax.random.permutation(key, blocks)[block_of(target)]
    other_side = (block_of(target) + blocks // 2) % blocks
    return jnp.where((block_of(source) == first) | (block_of(source) == other_side), factor * values, values)


def steps_of(key, extent, cuts, smallest, high):
    factor_of = 1.0
    for dim, blocks in cuts:
        draws = jax.random.uniform(jax.random.fold_in(jax.random.fold_in(key, 6), dim), (blocks,), jnp.float32, smallest / len(cuts), high / len(cuts))
        factor_of = factor_of * jnp.repeat(jnp.exp(draws), extent[dim] // blocks).reshape((-1,) + (1,) * (len(extent) - 1 - dim))
    return factor_of


def normal_values(stream_key, shape, scale, bound, cuts=(), held_as=jnp.bfloat16):
    entries = jax.random.normal(stream_key, shape, jnp.float32) * scale
    if len(cuts) > 0:
        entries = steps_of(stream_key, shape, cuts, -0.22, 0.18) * entries
    return jnp.clip(entries, min=-bound, max=bound).astype(held_as)


def heavy_noise(rng, extent, scale, bound, cuts, heavy, kind=jnp.bfloat16):
    result = scale * jax.random.normal(rng, extent, jnp.float32)
    if cuts:
        result = result * steps_of(rng, extent, cuts, -0.22, 0.18)
    return jnp.clip(strengthened(result, jax.random.fold_in(rng, 3), *heavy), -bound, bound).astype(kind)


def setup_inputs(seed: int = 0) -> dict:
    arg_keys = jax.random.split(jax.random.key(seed), 7)
    residual = heavy_noise(arg_keys[0], (N_GRP, N_SUB, ROWS, K), 1.0, 6.0, ((0, 4), (1, 8)), (1, 3, 8, 2.0))
    inverse_blocks = normal_values(arg_keys[1], (N_GRP, N_SUB, ROWS, EXT), EXT ** -0.5, 0.15625, ((0, 4), (1, 8)))
    operator_tiles = normal_values(arg_keys[2], (N_GRP, N_SUB, RB, NNZB, TILE, TILE), (NNZB * TILE) ** -0.5, 0.1875, ((0, 4), (1, 8)))
    column_blocks = with_ends(jax.random.randint(arg_keys[3], (N_GRP, N_SUB, RB, NNZB), 0, EB), jax.random.fold_in(arg_keys[3], 1), 0, EB - 1).astype(jnp.int32)
    coarse_basis = normal_values(arg_keys[4], (N_GRP, N_SUB, ROWS, C), 1.0, 6.0, ((0, 4), (1, 8)))
    face_rows = with_ends(jax.random.randint(arg_keys[5], (N_GRP, N_SUB, 4, OV), 0, ROWS), jax.random.fold_in(arg_keys[5], 1), 0, ROWS - 1).astype(jnp.int32)
    return dict(residual=residual, inverse_blocks=inverse_blocks, operator_tiles=operator_tiles, column_blocks=column_blocks, coarse_basis=coarse_basis, face_rows=face_rows)


def incoming(stacked, face_rows, grp_at, sub_at, face_index, present):
    grp_safe = jnp.clip(grp_at, 0, N_GRP - 1)
    sub_safe = jnp.clip(sub_at, 0, N_SUB - 1)
    picked_rows = face_rows[grp_safe, sub_safe, face_index]
    rows_sent = jnp.take(stacked[grp_safe, sub_safe], picked_rows, axis=0)
    return jnp.where(present, rows_sent, jnp.zeros_like(rows_sent))

def extend(stacked, face_rows, grp_at, sub_at):
    pieces = [stacked[grp_at, sub_at], incoming(stacked, face_rows, grp_at - 1, sub_at, 0, grp_at > 0), incoming(stacked, face_rows, grp_at + 1, sub_at, 1, grp_at < N_GRP - 1), incoming(stacked, face_rows, grp_at, sub_at - 1, 2, sub_at > 0), incoming(stacked, face_rows, grp_at, sub_at + 1, 3, sub_at < N_SUB - 1)]
    return jnp.concatenate(pieces, axis=0)

def reference(residual, inverse_blocks, operator_tiles, column_blocks, coarse_basis, face_rows):

    def visit_one(totals, device_at):
        galerkin_sum, rhs_sum = totals
        grp_at = device_at // N_SUB
        sub_at = device_at % N_SUB
        resid_ext = extend(residual, face_rows, grp_at, sub_at)
        basis_ext = extend(coarse_basis, face_rows, grp_at, sub_at)
        correction = jnp.dot(inverse_blocks[grp_at, sub_at], resid_ext, preferred_element_type=jnp.float32).astype(jnp.bfloat16)
        blocks = basis_ext.reshape(EXT // TILE, TILE, C)
        picked = jnp.take(blocks, column_blocks[grp_at, sub_at], axis=0)
        applied = jnp.einsum('bjtu,bjuc->btc', operator_tiles[grp_at, sub_at].astype(jnp.float32), picked.astype(jnp.float32), precision=lax.Precision.HIGHEST)
        applied = applied.reshape(ROWS, C).astype(jnp.bfloat16)
        own_basis = coarse_basis[grp_at, sub_at]
        galerkin_sum = galerkin_sum + jnp.dot(own_basis.T, applied, preferred_element_type=jnp.float32)
        rhs_sum = rhs_sum + jnp.dot(own_basis.T, residual[grp_at, sub_at], preferred_element_type=jnp.float32)
        return ((galerkin_sum, rhs_sum), correction)
    indices = jnp.arange(N_GRP * N_SUB, dtype=jnp.int32)
    start = (jnp.zeros((C, C), jnp.float32), jnp.zeros((C, K), jnp.float32))
    (galerkin_sum, rhs_sum), corrections = lax.scan(visit_one, start, indices)
    scaling = 1.0 / math.sqrt(ROWS * N_GRP * N_SUB)
    return (corrections.reshape(N_GRP, N_SUB, ROWS, K), galerkin_sum * scaling, rhs_sum * scaling)
```

```python
import functools
import math

import jax
import jax.numpy as jnp
from jax import lax
from jax.experimental import pallas as pl
from jax.experimental.pallas import tpu as pltpu
from jax.sharding import PartitionSpec as P

MESH = pl.DeviceIdType.MESH
F32 = jnp.float32
BF16 = jnp.bfloat16


def wide_dot(a, b):
    return jnp.dot(a, b, preferred_element_type=F32)


def dot_rows(a, b):
    return lax.dot_general(a, b, (((1,), (1,)), ((), ())), preferred_element_type=F32)


def kernel(
    n_grp, n_sub, width, scaling,
    col_ref, face_ref, basis_ref, resid_hbm, inv_hbm, tiles_hbm,
    fix_hbm, gal_ref, rhs_ref,
    resid, inv, tiles, pick, ext_send, ext, face_send, face_recv, total, fix,
    rhs_send, rhs_own, rhs_recv, sum_send, sum_recv,
    applied, gal, gal_recv, gal_sum, gal_sum_recv, gal_last, gal_full,
    in_sem, out_sem, ext_ss, ext_rs, face_ss, face_rs, rhs_ss, rhs_rs,
    sum_ss, sum_rs, gal_ss, gal_rs, gsum_ss, gsum_rs, glast_ss, glast_rs,
):
    g = lax.axis_index("grp")
    s = lax.axis_index("sub")
    rows, k = resid.shape
    coarse = basis_ref.shape[0]
    row_blocks, per_row, tile = tiles.shape[:3]
    own_blocks = rows // tile
    ov = face_ref.shape[1]
    chunks = k // width
    part = k // n_sub
    per_chunk = width // part
    gal_rows = gal_recv.shape[1]

    load_resid = pltpu.make_async_copy(resid_hbm, resid, in_sem.at[0])
    load_tiles = pltpu.make_async_copy(tiles_hbm, tiles, in_sem.at[1])
    load_inv = pltpu.make_async_copy(inv_hbm, inv, in_sem.at[2])
    load_resid.start()
    load_tiles.start()
    load_inv.start()

    barrier = pltpu.get_barrier_semaphore()

    @pl.loop(1, n_sub)
    def _(i):
        pl.semaphore_signal(barrier, inc=1, device_id=(g, lax.rem(s + i, n_sub)), device_id_type=MESH)

    @pl.loop(1, n_grp)
    def _(i):
        pl.semaphore_signal(barrier, inc=1, device_id=(lax.rem(g + i, n_grp), s), device_id_type=MESH)

    targets = ((g + 1, s), (g - 1, s), (g, s + 1), (g, s - 1))
    sends = (g < n_grp - 1, g > 0, s < n_sub - 1, s > 0)
    arrives = (g > 0, g < n_grp - 1, s > 0, s < n_sub - 1)

    def remote(src, dst, send_sem, recv_sem, device):
        return pltpu.make_async_remote_copy(
            src_ref=src, dst_ref=dst, send_sem=send_sem, recv_sem=recv_sem,
            device_id=device, device_id_type=MESH,
        )

    def ext_copy(f):
        return remote(ext_send.at[f], ext.at[own_blocks + f], ext_ss.at[f], ext_rs.at[f], targets[f])

    def face_copy(c, f):
        span = pl.ds(f * ov, ov)
        return remote(face_send.at[c, span], face_recv.at[c, span], face_ss.at[c, f], face_rs.at[c, f], targets[f])

    lanes = lax.broadcasted_iota(jnp.int32, (ov, tile), 1)
    for f in range(4):
        wanted = jnp.broadcast_to(face_ref[f:f + 1, :].astype(F32), (ov, ov)).T.astype(jnp.int32)
        for b in range(own_blocks):
            hit = wanted == lanes + b * tile
            pick[f * ov:(f + 1) * ov, b * tile:(b + 1) * tile] = jnp.where(hit, 1.0, 0.0).astype(BF16)
    basis = basis_ref[...]
    for f in range(4):
        ext_send[f] = dot_rows(basis, pick[f * ov:(f + 1) * ov, :]).astype(BF16)
    for b in range(own_blocks):
        ext[b] = basis_ref[:, b * tile:(b + 1) * tile]

    for f in range(4):
        @pl.when(jnp.logical_not(arrives[f]))
        def _():
            ext[own_blocks + f] = jnp.zeros((coarse, tile), BF16)
            face_recv[:, f * ov:(f + 1) * ov, :] = jnp.zeros((chunks, ov, width), BF16)

    pl.semaphore_wait(barrier, n_sub - 1 + n_grp - 1)
    for f in range(4):
        @pl.when(sends[f])
        def _():
            ext_copy(f).start()
    load_resid.wait()

    @pl.loop(0, chunks)
    def _(c):
        cols = pl.ds(pl.multiple_of(c * width, width), width)
        face_send[c] = wide_dot(pick[...], resid[:, cols]).astype(BF16)
        for f in range(4):
            @pl.when(sends[f])
            def _():
                face_copy(c, f).start()

    def rhs_copy(to):
        return remote(rhs_send.at[to], rhs_recv.at[s], rhs_ss.at[to], rhs_rs.at[s], (g, to))

    def rhs_from(frm):
        return remote(rhs_send.at[frm], rhs_recv.at[frm], rhs_ss.at[frm], rhs_rs.at[frm], (g, frm))

    @pl.loop(0, chunks)
    def _(c):
        cols = pl.ds(pl.multiple_of(c * width, width), width)
        term = wide_dot(basis_ref[...], resid[:, cols])
        for q in range(per_chunk):
            to = c * per_chunk + q
            piece = term[:, q * part:(q + 1) * part]
            rhs_send[to] = piece.astype(BF16)

            @pl.when(to == s)
            def _():
                rhs_own[...] = piece

            @pl.when(to != s)
            def _():
                rhs_copy(to).start()

    load_tiles.wait()
    for f in range(4):
        @pl.when(arrives[f])
        def _():
            ext_copy(f).wait_recv()

    @pl.loop(0, row_blocks)
    def _(b):
        row = jnp.concatenate([tiles[b, j] for j in range(per_row)], axis=1)
        picked = jnp.concatenate([ext[col_ref[b, j]] for j in range(per_row)], axis=1)
        applied[pl.ds(pl.multiple_of(b * tile, tile), tile), :] = dot_rows(row, picked).astype(BF16)

    gal[coarse:, :] = jnp.zeros((gal.shape[0] - coarse, coarse), F32)
    gal[:coarse, :] = wide_dot(basis_ref[...], applied[...])

    def gal_piece(i):
        return pl.ds(pl.multiple_of(i * gal_rows, 8), gal_rows)

    def gal_copy(to):
        return remote(gal.at[gal_piece(to)], gal_recv.at[s], gal_ss.at[to], gal_rs.at[s], (g, to))

    def gal_from(frm):
        return remote(gal.at[gal_piece(frm)], gal_recv.at[frm], gal_ss.at[frm], gal_rs.at[frm], (g, frm))

    @pl.loop(1, n_sub)
    def _(i):
        gal_copy(lax.rem(s + i, n_sub)).start()

    load_inv.wait()

    @pl.loop(0, chunks)
    def _(c):
        cols = pl.ds(pl.multiple_of(c * width, width), width)
        total[c] = wide_dot(inv[:, :rows], resid[:, cols])

    gal_sum[...] = gal[gal_piece(s), :]
    sum_send[...] = rhs_own[...]

    @pl.loop(1, n_sub)
    def _(i):
        frm = lax.rem(s + i, n_sub)
        gal_from(frm).wait_recv()
        gal_sum[...] += gal_recv[frm]
        rhs_from(frm).wait_recv()
        sum_send[...] += rhs_recv[frm].astype(F32)

    def sum_copies(i):
        to = lax.rem(g + i, n_grp)
        return (
            remote(sum_send, sum_recv.at[g], sum_ss.at[to], sum_rs.at[g], (to, s)),
            remote(gal_sum, gal_sum_recv.at[g], gsum_ss.at[to], gsum_rs.at[g], (to, s)),
        )

    def sum_from(i):
        frm = lax.rem(g + i, n_grp)
        return (
            remote(sum_send, sum_recv.at[frm], sum_ss.at[frm], sum_rs.at[frm], (frm, s)),
            remote(gal_sum, gal_sum_recv.at[frm], gsum_ss.at[frm], gsum_rs.at[frm], (frm, s)),
        )

    @pl.loop(1, n_grp)
    def _(i):
        for copy in reversed(sum_copies(i)):
            copy.start()

    def fix_out(c):
        cols = pl.ds(pl.multiple_of(c * width, width), width)
        return pltpu.make_async_copy(fix.at[c], fix_hbm.at[:, cols], out_sem.at[c])

    @pl.loop(0, chunks)
    def _(c):
        for f in range(4):
            @pl.when(arrives[f])
            def _():
                face_copy(c, f).wait_recv()
        fix[c] = (total[c] + wide_dot(inv[:, rows:], face_recv[c])).astype(BF16)
        fix_out(c).start()

    gal_last[...] = gal_sum[...]

    @pl.loop(1, n_grp)
    def _(i):
        sum_from(i)[1].wait_recv()
        gal_last[...] += gal_sum_recv[lax.rem(g + i, n_grp)]

    gal_last[...] = gal_last[...] * scaling

    def last_copy(to):
        return remote(gal_last, gal_full.at[gal_piece(s)], glast_ss.at[to], glast_rs.at[s], (g, to))

    def last_from(frm):
        return remote(gal_last, gal_full.at[gal_piece(frm)], glast_ss.at[frm], glast_rs.at[frm], (g, frm))

    @pl.loop(1, n_sub)
    def _(i):
        last_copy(lax.rem(s + i, n_sub)).start()

    gal_full[gal_piece(s), :] = gal_last[...]
    rhs_ref[...] = sum_send[...]

    @pl.loop(1, n_grp)
    def _(i):
        sum_from(i)[0].wait_recv()
        rhs_ref[...] += sum_recv[lax.rem(g + i, n_grp)]

    rhs_ref[...] = rhs_ref[...] * scaling

    @pl.loop(1, n_sub)
    def _(i):
        last_from(lax.rem(s + i, n_sub)).wait_recv()

    gal_ref[...] = gal_full[:coarse, :]

    for f in range(4):
        @pl.when(sends[f])
        def _():
            ext_copy(f).wait_send()

            @pl.loop(0, chunks)
            def _(c):
                face_copy(c, f).wait_send()

    @pl.loop(1, n_sub)
    def _(i):
        to = lax.rem(s + i, n_sub)
        rhs_copy(to).wait_send()
        gal_copy(to).wait_send()
        last_copy(to).wait_send()

    @pl.loop(1, n_grp)
    def _(i):
        for copy in sum_copies(i):
            copy.wait_send()

    @pl.loop(0, chunks)
    def _(c):
        fix_out(c).wait()


def local(n_grp, n_sub, residual, inverse_blocks, operator_tiles, column_blocks, coarse_basis, face_rows):
    resid = residual[0, 0]
    inv = inverse_blocks[0, 0]
    tiles = operator_tiles[0, 0]
    basis = jnp.swapaxes(coarse_basis[0, 0], 0, 1)
    faces = face_rows[0, 0]
    rows, k = resid.shape
    coarse = basis.shape[0]
    ov = faces.shape[1]
    tile = tiles.shape[-1]
    ext_blocks = inv.shape[1] // tile
    part = k // n_sub
    width = max(256, part)
    chunks = k // width
    gal_rows = -(-coarse // (8 * n_sub)) * 8
    scaling = 1.0 / math.sqrt(rows * n_grp * n_sub)
    dma = pltpu.SemaphoreType.DMA
    hbm = pl.BlockSpec(memory_space=pl.ANY)
    vmem = pl.BlockSpec(memory_space=pltpu.VMEM)
    fix, gal, rhs = pl.pallas_call(
        functools.partial(kernel, n_grp, n_sub, width, scaling),
        out_shape=(
            jax.ShapeDtypeStruct((rows, k), BF16),
            jax.ShapeDtypeStruct((coarse, coarse), F32),
            jax.ShapeDtypeStruct((coarse, part), F32),
        ),
        in_specs=[pl.BlockSpec(memory_space=pltpu.SMEM), vmem, vmem, hbm, hbm, hbm],
        out_specs=(hbm, vmem, vmem),
        scratch_shapes=[
            pltpu.VMEM(resid.shape, BF16),
            pltpu.VMEM(inv.shape, BF16),
            pltpu.VMEM(tiles.shape, BF16),
            pltpu.VMEM((4 * ov, rows), BF16),
            pltpu.VMEM((4, coarse, tile), BF16),
            pltpu.VMEM((ext_blocks, coarse, tile), BF16),
            pltpu.VMEM((chunks, 4 * ov, width), BF16),
            pltpu.VMEM((chunks, 4 * ov, width), BF16),
            pltpu.VMEM((chunks, rows, width), F32),
            pltpu.VMEM((chunks, rows, width), BF16),
            pltpu.VMEM((n_sub, coarse, part), BF16),
            pltpu.VMEM((coarse, part), F32),
            pltpu.VMEM((n_sub, coarse, part), BF16),
            pltpu.VMEM((coarse, part), F32),
            pltpu.VMEM((n_grp, coarse, part), F32),
            pltpu.VMEM((rows, coarse), BF16),
            pltpu.VMEM((n_sub * gal_rows, coarse), F32),
            pltpu.VMEM((n_sub, gal_rows, coarse), F32),
            pltpu.VMEM((gal_rows, coarse), F32),
            pltpu.VMEM((n_grp, gal_rows, coarse), F32),
            pltpu.VMEM((gal_rows, coarse), F32),
            pltpu.VMEM((n_sub * gal_rows, coarse), F32),
            dma((3,)),
            dma((chunks,)),
            dma((4,)),
            dma((4,)),
            dma((chunks, 4)),
            dma((chunks, 4)),
            dma((n_sub,)),
            dma((n_sub,)),
            dma((n_grp,)),
            dma((n_grp,)),
            dma((n_sub,)),
            dma((n_sub,)),
            dma((n_grp,)),
            dma((n_grp,)),
            dma((n_sub,)),
            dma((n_sub,)),
        ],
        compiler_params=pltpu.CompilerParams(
            collective_id=0, has_side_effects=True, vmem_limit_bytes=60 * 1024 * 1024
        ),
    )(column_blocks[0, 0], faces, basis, resid, inv, tiles)
    return fix[None, None], gal, rhs


def solution(mesh):
    return jax.shard_map(
        functools.partial(local, mesh.shape["grp"], mesh.shape["sub"]),
        mesh=mesh,
        in_specs=(
            P("grp", "sub", None, None),
            P("grp", "sub", None, None),
            P("grp", "sub", None, None, None, None),
            P("grp", "sub", None, None),
            P("grp", "sub", None, None),
            P("grp", "sub", None, None),
        ),
        out_specs=(P("grp", "sub", None, None), P(), P(None, "sub")),
        check_vma=False,
    )
```

```python
import functools
import math

import jax
import jax.numpy as jnp
from jax import lax
from jax.experimental import pallas as pl
from jax.experimental.pallas import tpu as pltpu
from jax.sharding import PartitionSpec as P

MESH = pl.DeviceIdType.MESH
F32 = jnp.float32
BF16 = jnp.bfloat16


def wide_dot(a, b):
    return jnp.dot(a, b, preferred_element_type=F32)


def dot_rows(a, b):
    return lax.dot_general(a, b, (((1,), (1,)), ((), ())), preferred_element_type=F32)


def kernel(
    n_grp, n_sub, width, scaling,
    col_ref, face_ref, basis_ref, resid_hbm, inv_hbm, tiles_hbm,
    fix_hbm, gal_ref, rhs_ref,
    resid, inv, tiles, pick, ext_send, ext, face_send, face_recv, relay, total, fix,
    keep, pair_send, pair_recv, rhs_send, rhs_recv, sum_send, sum_recv, sum_last, sum_full,
    applied, gal, gal_pair, gal_both, gal_recv, gal_sum, gal_sum_recv, gal_last, gal_full,
    in_sem, resid_sem, out_sem, ext_ss, ext_rs, face_ss, face_rs, relay_ss, relay_rs,
    pair_ss, pair_rs, gpair_ss, gpair_rs, rhs_ss, rhs_rs,
    sum_ss, sum_rs, last_ss, last_rs, gal_ss, gal_rs, gsum_ss, gsum_rs, glast_ss, glast_rs,
):
    g = lax.axis_index("grp")
    s = lax.axis_index("sub")
    chip, core = s // 2, lax.rem(s, 2)
    partner = s + 1 - 2 * core
    chips = n_sub // 2
    chunks, rows, _ = resid.shape
    coarse = basis_ref.shape[0]
    row_blocks, per_row, tile = tiles.shape[:3]
    own_blocks = rows // tile
    ov = face_ref.shape[1]
    part = chunks * width // n_sub
    per_chunk = width // part
    gal_rows = gal_recv.shape[1]
    sum_rows = sum_recv.shape[1]
    relayed = n_grp == 4

    def load_resid(c):
        cols = pl.ds(pl.multiple_of(c * width, width), width)
        return pltpu.make_async_copy(resid_hbm.at[:, cols], resid.at[c], resid_sem.at[c])

    load_tiles = pltpu.make_async_copy(tiles_hbm, tiles, in_sem.at[0])
    load_inv = pltpu.make_async_copy(inv_hbm, inv, in_sem.at[1])

    @pl.loop(0, chunks)
    def _(c):
        load_resid(c).start()

    load_tiles.start()
    load_inv.start()

    barrier = pltpu.get_barrier_semaphore()

    @pl.loop(1, n_sub)
    def _(i):
        pl.semaphore_signal(barrier, inc=1, device_id=(g, lax.rem(s + i, n_sub)), device_id_type=MESH)

    @pl.loop(1, n_grp)
    def _(i):
        pl.semaphore_signal(barrier, inc=1, device_id=(lax.rem(g + i, n_grp), s), device_id_type=MESH)

    targets = ((g + 1, s), (g - 1, s), (g, s + 1), (g, s - 1))
    sends = (g < n_grp - 1, g > 0, s < n_sub - 1, s > 0)
    arrives = (g > 0, g < n_grp - 1, s > 0, s < n_sub - 1)

    def remote(src, dst, send_sem, recv_sem, device):
        return pltpu.make_async_remote_copy(
            src_ref=src, dst_ref=dst, send_sem=send_sem, recv_sem=recv_sem,
            device_id=device, device_id_type=MESH,
        )

    def ext_copy(f):
        return remote(ext_send.at[f], ext.at[own_blocks + f], ext_ss.at[f], ext_rs.at[f], targets[f])

    def face_copy(c, f, far=False):
        span = pl.ds(f * ov, ov)
        if far:
            way = (n_grp - 1) * (lax.rem(c + f, 2))
            return remote(face_send.at[c, span], relay.at[c], face_ss.at[c, f], relay_rs.at[c], (way, s))
        return remote(face_send.at[c, span], face_recv.at[c, span], face_ss.at[c, f], face_rs.at[c, f], targets[f])

    def forward(c, f):
        span = pl.ds(f * ov, ov)
        return remote(relay.at[c], face_recv.at[c, span], relay_ss.at[c], face_rs.at[c, f], (2 - f, s))

    def far_face(f):
        return (g == 1 + f) if relayed and f < 2 else None

    def face_start(c, f):
        far = far_face(f)
        if far is None:
            @pl.when(sends[f])
            def _():
                face_copy(c, f).start()
        else:
            @pl.when(far)
            def _():
                face_copy(c, f, True).start()

            @pl.when(jnp.logical_and(sends[f], jnp.logical_not(far)))
            def _():
                face_copy(c, f).start()

    def when_relaying(c, do):
        if relayed:
            turn = lax.rem(c + jnp.where(g == 3, 1, 0), 2)
            for f in range(2):
                @pl.when(jnp.logical_and(jnp.logical_or(g == 0, g == 3), turn == f))
                def _():
                    do(forward(c, f))

    lanes = lax.broadcasted_iota(jnp.int32, (ov, tile), 1)
    for f in range(4):
        wanted = jnp.broadcast_to(face_ref[f:f + 1, :].astype(F32), (ov, ov)).T.astype(jnp.int32)
        for b in range(own_blocks):
            hit = wanted == lanes + b * tile
            pick[f * ov:(f + 1) * ov, b * tile:(b + 1) * tile] = jnp.where(hit, 1.0, 0.0).astype(BF16)
    basis = basis_ref[...]
    for f in range(4):
        ext_send[f] = dot_rows(basis, pick[f * ov:(f + 1) * ov, :]).astype(BF16)
    for b in range(own_blocks):
        ext[b] = basis_ref[:, b * tile:(b + 1) * tile]

    for f in range(4):
        @pl.when(jnp.logical_not(arrives[f]))
        def _():
            ext[own_blocks + f] = jnp.zeros((coarse, tile), BF16)
            face_recv[:, f * ov:(f + 1) * ov, :] = jnp.zeros((chunks, ov, width), BF16)

    pl.semaphore_wait(barrier, n_sub - 1 + n_grp - 1)
    for f in range(4):
        @pl.when(sends[f])
        def _():
            ext_copy(f).start()

    @pl.loop(0, chunks)
    def _(c):
        load_resid(c).wait()
        face_send[c] = wide_dot(pick[...], resid[c]).astype(BF16)
        for f in range(4):
            face_start(c, f)

    def pair_copy(i):
        return remote(pair_send.at[i], pair_recv.at[i], pair_ss.at[i], pair_rs.at[i], (g, partner))

    @pl.loop(0, chunks)
    def _(c):
        term = wide_dot(basis_ref[...], resid[c])
        for q in range(per_chunk):
            to = c * per_chunk + q
            piece = term[:, q * part:(q + 1) * part]

            @pl.when(lax.rem(to, 2) == core)
            def _():
                keep[to // 2] = piece

            @pl.when(lax.rem(to, 2) != core)
            def _():
                pair_send[to // 2] = piece
                pair_copy(to // 2).start()

    load_tiles.wait()
    for f in range(4):
        @pl.when(arrives[f])
        def _():
            ext_copy(f).wait_recv()

    @pl.loop(0, row_blocks)
    def _(b):
        row = jnp.concatenate([tiles[b, j] for j in range(per_row)], axis=1)
        picked = jnp.concatenate([ext[col_ref[b, j]] for j in range(per_row)], axis=1)
        applied[pl.ds(pl.multiple_of(b * tile, tile), tile), :] = dot_rows(row, picked).astype(BF16)

    gal[coarse:, :] = jnp.zeros((gal.shape[0] - coarse, coarse), F32)
    gal[:coarse, :] = wide_dot(basis_ref[...], applied[...])

    gal_swap = remote(gal, gal_pair, gpair_ss.at[0], gpair_rs.at[0], (g, partner))
    gal_swap.start()
    load_inv.wait()

    @pl.loop(0, chunks // 2)
    def _(c):
        total[c] = wide_dot(inv[:, :rows], resid[c])

    def rhs_copy(i):
        to = lax.rem(chip + i, chips)
        return remote(rhs_send.at[to], rhs_recv.at[chip], rhs_ss.at[to], rhs_rs.at[chip], (g, to * 2 + core))

    def rhs_from(i):
        frm = lax.rem(chip + i, chips)
        return remote(rhs_send.at[frm], rhs_recv.at[frm], rhs_ss.at[frm], rhs_rs.at[frm], (g, frm * 2 + core))

    def gal_piece(i):
        return pl.ds(pl.multiple_of(i * gal_rows, 8), gal_rows)

    def gal_copy(i):
        to = lax.rem(chip + i, chips)
        piece = gal_both.at[gal_piece(to * 2 + core)]
        return remote(piece, gal_recv.at[chip], gal_ss.at[to], gal_rs.at[chip], (g, to * 2 + core))

    def gal_from(i):
        frm = lax.rem(chip + i, chips)
        piece = gal_both.at[gal_piece(frm * 2 + core)]
        return remote(piece, gal_recv.at[frm], gal_ss.at[frm], gal_rs.at[frm], (g, frm * 2 + core))

    gal_swap.wait_recv()
    gal_both[...] = gal[...] + gal_pair[...]

    @pl.loop(1, chips)
    def _(i):
        gal_copy(i).start()

    @pl.loop(1, chips)
    def _(i):
        to = lax.rem(chip + i, chips)
        pair_copy(to).wait_recv()
        rhs_send[to] = (keep[to] + pair_recv[to]).astype(BF16)
        rhs_copy(i).start()

    pair_copy(chip).wait_recv()
    sum_send[:coarse, :] = keep[chip] + pair_recv[chip]
    if sum_send.shape[0] > coarse:
        sum_send[coarse:, :] = jnp.zeros((sum_send.shape[0] - coarse, part), F32)
    gal_sum[...] = gal_both[gal_piece(s), :]

    @pl.loop(chunks // 2, chunks)
    def _(c):
        total[c] = wide_dot(inv[:, :rows], resid[c])

    def fix_out(c):
        cols = pl.ds(pl.multiple_of(c * width, width), width)
        return pltpu.make_async_copy(fix.at[c], fix_hbm.at[:, cols], out_sem.at[c])

    def finish(c):
        def pass_on(copy):
            remote(relay.at[c], relay.at[c], relay_ss.at[c], relay_rs.at[c], (1, s)).wait_recv()
            copy.start()

        when_relaying(c, pass_on)
        for f in range(4):
            @pl.when(arrives[f])
            def _():
                face_copy(c, f).wait_recv()
        fix[c] = (total[c] + wide_dot(inv[:, rows:], face_recv[c])).astype(BF16)
        fix_out(c).start()

    late = chunks - chunks // 4

    @pl.loop(0, late)
    def _(c):
        finish(c)

    def gsum_copy(i):
        to = lax.rem(g + i, n_grp)
        return remote(gal_sum, gal_sum_recv.at[g], gsum_ss.at[to], gsum_rs.at[g], (to, s))

    def gsum_from(i):
        frm = lax.rem(g + i, n_grp)
        return remote(gal_sum, gal_sum_recv.at[frm], gsum_ss.at[frm], gsum_rs.at[frm], (frm, s))

    def sum_piece(i):
        return pl.ds(pl.multiple_of(i * sum_rows, 8), sum_rows)

    def sum_copy(i):
        to = lax.rem(g + i, n_grp)
        return remote(sum_send.at[sum_piece(to)], sum_recv.at[g], sum_ss.at[to], sum_rs.at[g], (to, s))

    def sum_from(i):
        frm = lax.rem(g + i, n_grp)
        return remote(sum_send.at[sum_piece(frm)], sum_recv.at[frm], sum_ss.at[frm], sum_rs.at[frm], (frm, s))

    def last_copy(i):
        to = lax.rem(g + i, n_grp)
        return remote(sum_last, sum_full.at[sum_piece(g)], last_ss.at[to], last_rs.at[g], (to, s))

    def last_from(i):
        frm = lax.rem(g + i, n_grp)
        return remote(sum_last, sum_full.at[sum_piece(frm)], last_ss.at[frm], last_rs.at[frm], (frm, s))

    def glast_copy(i):
        to = lax.rem(s + i, n_sub)
        return remote(gal_last, gal_full.at[gal_piece(s)], glast_ss.at[to], glast_rs.at[s], (g, to))

    def glast_from(i):
        frm = lax.rem(s + i, n_sub)
        return remote(gal_last, gal_full.at[gal_piece(frm)], glast_ss.at[frm], glast_rs.at[frm], (g, frm))

    @pl.loop(1, chips)
    def _(i):
        gal_from(i).wait_recv()
        gal_sum[...] += gal_recv[lax.rem(chip + i, chips)]

    @pl.loop(1, n_grp)
    def _(i):
        gsum_copy(i).start()

    @pl.loop(1, chips)
    def _(i):
        rhs_from(i).wait_recv()
        sum_send[:coarse, :] += rhs_recv[lax.rem(chip + i, chips)].astype(F32)

    @pl.loop(1, n_grp)
    def _(i):
        sum_copy(i).start()

    @pl.loop(late, chunks)
    def _(c):
        finish(c)

    gal_last[...] = gal_sum[...]

    @pl.loop(1, n_grp)
    def _(i):
        gsum_from(i).wait_recv()
        gal_last[...] += gal_sum_recv[lax.rem(g + i, n_grp)]

    gal_last[...] = gal_last[...] * scaling

    @pl.loop(1, n_sub)
    def _(i):
        glast_copy(i).start()

    sum_last[...] = sum_send[sum_piece(g), :]

    @pl.loop(1, n_grp)
    def _(i):
        sum_from(i).wait_recv()
        sum_last[...] += sum_recv[lax.rem(g + i, n_grp)]

    sum_last[...] = sum_last[...] * scaling

    @pl.loop(1, n_grp)
    def _(i):
        last_copy(i).start()

    gal_full[gal_piece(s), :] = gal_last[...]
    sum_full[sum_piece(g), :] = sum_last[...]

    @pl.loop(1, n_sub)
    def _(i):
        glast_from(i).wait_recv()

    gal_ref[...] = gal_full[:coarse, :]

    @pl.loop(1, n_grp)
    def _(i):
        last_from(i).wait_recv()

    rhs_ref[...] = sum_full[:coarse, :]

    for f in range(4):
        @pl.when(sends[f])
        def _():
            ext_copy(f).wait_send()

            @pl.loop(0, chunks)
            def _(c):
                face_copy(c, f).wait_send()

    @pl.loop(0, chunks)
    def _(c):
        when_relaying(c, lambda copy: copy.wait_send())
        fix_out(c).wait()

    gal_swap.wait_send()

    @pl.loop(0, chips)
    def _(i):
        pair_copy(i).wait_send()

    @pl.loop(1, chips)
    def _(i):
        rhs_copy(i).wait_send()
        gal_copy(i).wait_send()

    @pl.loop(1, n_sub)
    def _(i):
        glast_copy(i).wait_send()

    @pl.loop(1, n_grp)
    def _(i):
        gsum_copy(i).wait_send()
        sum_copy(i).wait_send()
        last_copy(i).wait_send()


def local(n_grp, n_sub, residual, inverse_blocks, operator_tiles, column_blocks, coarse_basis, face_rows):
    resid = residual[0, 0]
    inv = inverse_blocks[0, 0]
    tiles = operator_tiles[0, 0]
    basis = jnp.swapaxes(coarse_basis[0, 0], 0, 1)
    faces = face_rows[0, 0]
    rows, k = resid.shape
    coarse = basis.shape[0]
    ov = faces.shape[1]
    tile = tiles.shape[-1]
    ext_blocks = inv.shape[1] // tile
    part = k // n_sub
    width = max(256, part)
    chunks = k // width
    gal_rows = -(-coarse // (8 * n_sub)) * 8
    sum_rows = -(-coarse // (8 * n_grp)) * 8
    chips = n_sub // 2
    scaling = 1.0 / math.sqrt(rows * n_grp * n_sub)
    dma = pltpu.SemaphoreType.DMA
    hbm = pl.BlockSpec(memory_space=pl.ANY)
    vmem = pl.BlockSpec(memory_space=pltpu.VMEM)
    fix, gal, rhs = pl.pallas_call(
        functools.partial(kernel, n_grp, n_sub, width, scaling),
        out_shape=(
            jax.ShapeDtypeStruct((rows, k), BF16),
            jax.ShapeDtypeStruct((coarse, coarse), F32),
            jax.ShapeDtypeStruct((coarse, part), F32),
        ),
        in_specs=[pl.BlockSpec(memory_space=pltpu.SMEM), vmem, vmem, hbm, hbm, hbm],
        out_specs=(hbm, vmem, vmem),
        scratch_shapes=[
            pltpu.VMEM((chunks, rows, width), BF16),
            pltpu.VMEM(inv.shape, BF16),
            pltpu.VMEM(tiles.shape, BF16),
            pltpu.VMEM((4 * ov, rows), BF16),
            pltpu.VMEM((4, coarse, tile), BF16),
            pltpu.VMEM((ext_blocks, coarse, tile), BF16),
            pltpu.VMEM((chunks, 4 * ov, width), BF16),
            pltpu.VMEM((chunks, 4 * ov, width), BF16),
            pltpu.VMEM((chunks, ov, width), BF16),
            pltpu.VMEM((chunks, rows, width), F32),
            pltpu.VMEM((chunks, rows, width), BF16),
            pltpu.VMEM((chips, coarse, part), F32),
            pltpu.VMEM((chips, coarse, part), F32),
            pltpu.VMEM((chips, coarse, part), F32),
            pltpu.VMEM((chips, coarse, part), BF16),
            pltpu.VMEM((chips, coarse, part), BF16),
            pltpu.VMEM((n_grp * sum_rows, part), F32),
            pltpu.VMEM((n_grp, sum_rows, part), F32),
            pltpu.VMEM((sum_rows, part), F32),
            pltpu.VMEM((n_grp * sum_rows, part), F32),
            pltpu.VMEM((rows, coarse), BF16),
            pltpu.VMEM((n_sub * gal_rows, coarse), F32),
            pltpu.VMEM((n_sub * gal_rows, coarse), F32),
            pltpu.VMEM((n_sub * gal_rows, coarse), F32),
            pltpu.VMEM((chips, gal_rows, coarse), F32),
            pltpu.VMEM((gal_rows, coarse), F32),
            pltpu.VMEM((n_grp, gal_rows, coarse), F32),
            pltpu.VMEM((gal_rows, coarse), F32),
            pltpu.VMEM((n_sub * gal_rows, coarse), F32),
            dma((2,)),
            dma((chunks,)),
            dma((chunks,)),
            dma((4,)),
            dma((4,)),
            dma((chunks, 4)),
            dma((chunks, 4)),
            dma((chunks,)),
            dma((chunks,)),
            dma((chips,)),
            dma((chips,)),
            dma((1,)),
            dma((1,)),
            dma((chips,)),
            dma((chips,)),
            dma((n_grp,)),
            dma((n_grp,)),
            dma((n_grp,)),
            dma((n_grp,)),
            dma((chips,)),
            dma((chips,)),
            dma((n_grp,)),
            dma((n_grp,)),
            dma((n_sub,)),
            dma((n_sub,)),
        ],
        compiler_params=pltpu.CompilerParams(
            collective_id=0, has_side_effects=True, vmem_limit_bytes=60 * 1024 * 1024
        ),
    )(column_blocks[0, 0], faces, basis, resid, inv, tiles)
    return fix[None, None], gal, rhs


def solution(mesh):
    return jax.shard_map(
        functools.partial(local, mesh.shape["grp"], mesh.shape["sub"]),
        mesh=mesh,
        in_specs=(
            P("grp", "sub", None, None),
            P("grp", "sub", None, None),
            P("grp", "sub", None, None, None, None),
            P("grp", "sub", None, None),
            P("grp", "sub", None, None),
            P("grp", "sub", None, None),
        ),
        out_specs=(P("grp", "sub", None, None), P(), P(None, "sub")),
        check_vma=False,
    )
```

```python
import functools
import math

import jax
import jax.numpy as jnp
from jax import lax
from jax.experimental import pallas as pl
from jax.experimental.pallas import tpu as pltpu
from jax.sharding import PartitionSpec as P

MESH = pl.DeviceIdType.MESH
F32 = jnp.float32
BF16 = jnp.bfloat16


def wide_dot(a, b):
    return jnp.dot(a, b, preferred_element_type=F32)


def dot_rows(a, b):
    return lax.dot_general(a, b, (((1,), (1,)), ((), ())), preferred_element_type=F32)


def kernel(
    n_grp, n_sub, width, scaling,
    col_ref, face_ref, basis_ref, resid_hbm, inv_hbm, tiles_hbm,
    fix_ref, gal_ref, rhs_ref,
    resid, inv, tiles, pick, ext_send, ext, face_send, face_recv, relay, total,
    keep, pair_send, pair_recv, rhs_send, rhs_recv, sum_send, sum_recv, sum_last, sum_full,
    applied, gal, gal_pair, gal_both, gal_recv, gal_sum, gal_sum_recv, gal_last, gal_full,
    in_sem, resid_sem, ext_ss, ext_rs, face_ss, face_rs, relay_ss, relay_rs,
    pair_ss, pair_rs, gpair_ss, gpair_rs, rhs_ss, rhs_rs,
    sum_ss, sum_rs, last_ss, last_rs, gal_ss, gal_rs, gsum_ss, gsum_rs, glast_ss, glast_rs,
):
    g = lax.axis_index("grp")
    s = lax.axis_index("sub")
    chip, core = s // 2, lax.rem(s, 2)
    partner = s + 1 - 2 * core
    chips = n_sub // 2
    chunks, rows, _ = resid.shape
    coarse = basis_ref.shape[0]
    row_blocks, per_row, tile = tiles.shape[:3]
    own_blocks = rows // tile
    ov = face_ref.shape[1]
    part = chunks * width // n_sub
    per_chunk = width // part
    gal_rows = gal_recv.shape[1]
    sum_rows = sum_recv.shape[1]
    relayed = n_grp == 4

    def load_resid(c):
        cols = pl.ds(pl.multiple_of(c * width, width), width)
        return pltpu.make_async_copy(resid_hbm.at[:, cols], resid.at[c], resid_sem.at[c])

    load_tiles = pltpu.make_async_copy(tiles_hbm, tiles, in_sem.at[0])
    load_inv = pltpu.make_async_copy(inv_hbm, inv, in_sem.at[1])

    @pl.loop(0, chunks)
    def _(c):
        load_resid(c).start()

    load_tiles.start()
    load_inv.start()

    barrier = pltpu.get_barrier_semaphore()

    @pl.loop(1, n_sub)
    def _(i):
        pl.semaphore_signal(barrier, inc=1, device_id=(g, lax.rem(s + i, n_sub)), device_id_type=MESH)

    @pl.loop(1, n_grp)
    def _(i):
        pl.semaphore_signal(barrier, inc=1, device_id=(lax.rem(g + i, n_grp), s), device_id_type=MESH)

    targets = ((g + 1, s), (g - 1, s), (g, s + 1), (g, s - 1))
    sends = (g < n_grp - 1, g > 0, s < n_sub - 1, s > 0)
    arrives = (g > 0, g < n_grp - 1, s > 0, s < n_sub - 1)

    def remote(src, dst, send_sem, recv_sem, device):
        return pltpu.make_async_remote_copy(
            src_ref=src, dst_ref=dst, send_sem=send_sem, recv_sem=recv_sem,
            device_id=device, device_id_type=MESH,
        )

    def ext_copy(f):
        return remote(ext_send.at[f], ext.at[own_blocks + f], ext_ss.at[f], ext_rs.at[f], targets[f])

    def face_copy(c, f, far=False):
        span = pl.ds(f * ov, ov)
        if far:
            way = (n_grp - 1) * (lax.rem(c + f, 2))
            return remote(face_send.at[c, span], relay.at[c], face_ss.at[c, f], relay_rs.at[c], (way, s))
        return remote(face_send.at[c, span], face_recv.at[c, span], face_ss.at[c, f], face_rs.at[c, f], targets[f])

    def forward(c, f):
        span = pl.ds(f * ov, ov)
        return remote(relay.at[c], face_recv.at[c, span], relay_ss.at[c], face_rs.at[c, f], (2 - f, s))

    def far_face(f):
        return (g == 1 + f) if relayed and f < 2 else None

    def face_start(c, f):
        far = far_face(f)
        if far is None:
            @pl.when(sends[f])
            def _():
                face_copy(c, f).start()
        else:
            @pl.when(far)
            def _():
                face_copy(c, f, True).start()

            @pl.when(jnp.logical_and(sends[f], jnp.logical_not(far)))
            def _():
                face_copy(c, f).start()

    def when_relaying(c, do):
        if relayed:
            turn = lax.rem(c + jnp.where(g == 3, 1, 0), 2)
            for f in range(2):
                @pl.when(jnp.logical_and(jnp.logical_or(g == 0, g == 3), turn == f))
                def _():
                    do(forward(c, f))

    lanes = lax.broadcasted_iota(jnp.int32, (ov, tile), 1)
    for f in range(4):
        wanted = jnp.broadcast_to(face_ref[f:f + 1, :].astype(F32), (ov, ov)).T.astype(jnp.int32)
        for b in range(own_blocks):
            hit = wanted == lanes + b * tile
            pick[f * ov:(f + 1) * ov, b * tile:(b + 1) * tile] = jnp.where(hit, 1.0, 0.0).astype(BF16)
    basis = basis_ref[...]
    for f in range(4):
        ext_send[f] = dot_rows(basis, pick[f * ov:(f + 1) * ov, :]).astype(BF16)
    for b in range(own_blocks):
        ext[b] = basis_ref[:, b * tile:(b + 1) * tile]

    for f in range(4):
        @pl.when(jnp.logical_not(arrives[f]))
        def _():
            ext[own_blocks + f] = jnp.zeros((coarse, tile), BF16)
            face_recv[:, f * ov:(f + 1) * ov, :] = jnp.zeros((chunks, ov, width), BF16)

    pl.semaphore_wait(barrier, n_sub - 1 + n_grp - 1)
    for f in range(4):
        @pl.when(sends[f])
        def _():
            ext_copy(f).start()

    def pair_copy(i):
        return remote(pair_send.at[i], pair_recv.at[i], pair_ss.at[i], pair_rs.at[i], (g, partner))

    @pl.loop(0, chunks)
    def _(c):
        load_resid(c).wait()
        face_send[c] = wide_dot(pick[...], resid[c]).astype(BF16)
        for f in range(4):
            face_start(c, f)
        term = wide_dot(basis_ref[...], resid[c])
        for q in range(per_chunk):
            to = c * per_chunk + q
            piece = term[:, q * part:(q + 1) * part]

            @pl.when(lax.rem(to, 2) == core)
            def _():
                keep[to // 2] = piece

            @pl.when(lax.rem(to, 2) != core)
            def _():
                pair_send[to // 2] = piece
                pair_copy(to // 2).start()

    load_tiles.wait()
    for f in range(4):
        @pl.when(arrives[f])
        def _():
            ext_copy(f).wait_recv()

    @pl.loop(0, row_blocks)
    def _(b):
        row = jnp.concatenate([tiles[b, j] for j in range(per_row)], axis=1)
        picked = jnp.concatenate([ext[col_ref[b, j]] for j in range(per_row)], axis=1)
        applied[pl.ds(pl.multiple_of(b * tile, tile), tile), :] = dot_rows(row, picked).astype(BF16)

    gal[coarse:, :] = jnp.zeros((gal.shape[0] - coarse, coarse), F32)
    gal[:coarse, :] = wide_dot(basis_ref[...], applied[...])

    gal_swap = remote(gal, gal_pair, gpair_ss.at[0], gpair_rs.at[0], (g, partner))
    gal_swap.start()
    def rhs_copy(i):
        to = lax.rem(chip + i, chips)
        return remote(rhs_send.at[to], rhs_recv.at[chip], rhs_ss.at[to], rhs_rs.at[chip], (g, to * 2 + core))

    def rhs_from(i):
        frm = lax.rem(chip + i, chips)
        return remote(rhs_send.at[frm], rhs_recv.at[frm], rhs_ss.at[frm], rhs_rs.at[frm], (g, frm * 2 + core))

    @pl.loop(1, chips)
    def _(i):
        to = lax.rem(chip + i, chips)
        pair_copy(to).wait_recv()
        rhs_send[to] = (keep[to] + pair_recv[to]).astype(BF16)
        rhs_copy(i).start()

    pair_copy(chip).wait_recv()
    sum_send[:coarse, :] = keep[chip] + pair_recv[chip]
    if sum_send.shape[0] > coarse:
        sum_send[coarse:, :] = jnp.zeros((sum_send.shape[0] - coarse, part), F32)
    load_inv.wait()

    @pl.loop(0, chunks // 2)
    def _(c):
        total[c] = wide_dot(inv[:, :rows], resid[c])

    def gal_piece(i):
        return pl.ds(pl.multiple_of(i * gal_rows, 8), gal_rows)

    def gal_copy(i):
        to = lax.rem(chip + i, chips)
        piece = gal_both.at[gal_piece(to * 2 + core)]
        return remote(piece, gal_recv.at[chip], gal_ss.at[to], gal_rs.at[chip], (g, to * 2 + core))

    def gal_from(i):
        frm = lax.rem(chip + i, chips)
        piece = gal_both.at[gal_piece(frm * 2 + core)]
        return remote(piece, gal_recv.at[frm], gal_ss.at[frm], gal_rs.at[frm], (g, frm * 2 + core))

    gal_swap.wait_recv()
    gal_both[...] = gal[...] + gal_pair[...]

    @pl.loop(1, chips)
    def _(i):
        gal_copy(i).start()

    gal_sum[...] = gal_both[gal_piece(s), :]

    @pl.loop(chunks // 2, chunks)
    def _(c):
        total[c] = wide_dot(inv[:, :rows], resid[c])

    def finish(c):
        def pass_on(copy):
            remote(relay.at[c], relay.at[c], relay_ss.at[c], relay_rs.at[c], (1, s)).wait_recv()
            copy.start()

        when_relaying(c, pass_on)
        for f in range(4):
            @pl.when(arrives[f])
            def _():
                face_copy(c, f).wait_recv()
        cols = pl.ds(pl.multiple_of(c * width, width), width)
        fix_ref[:, cols] = (total[c] + wide_dot(inv[:, rows:], face_recv[c])).astype(BF16)

    late = chunks - chunks // 4

    @pl.loop(0, late)
    def _(c):
        finish(c)

    def gsum_copy(i):
        to = lax.rem(g + i, n_grp)
        return remote(gal_sum, gal_sum_recv.at[g], gsum_ss.at[to], gsum_rs.at[g], (to, s))

    def gsum_from(i):
        frm = lax.rem(g + i, n_grp)
        return remote(gal_sum, gal_sum_recv.at[frm], gsum_ss.at[frm], gsum_rs.at[frm], (frm, s))

    def sum_piece(i):
        return pl.ds(pl.multiple_of(i * sum_rows, 8), sum_rows)

    def sum_copy(i):
        to = lax.rem(g + i, n_grp)
        return remote(sum_send.at[sum_piece(to)], sum_recv.at[g], sum_ss.at[to], sum_rs.at[g], (to, s))

    def sum_from(i):
        frm = lax.rem(g + i, n_grp)
        return remote(sum_send.at[sum_piece(frm)], sum_recv.at[frm], sum_ss.at[frm], sum_rs.at[frm], (frm, s))

    def last_copy(i):
        to = lax.rem(g + i, n_grp)
        return remote(sum_last, sum_full.at[sum_piece(g)], last_ss.at[to], last_rs.at[g], (to, s))

    def last_from(i):
        frm = lax.rem(g + i, n_grp)
        return remote(sum_last, sum_full.at[sum_piece(frm)], last_ss.at[frm], last_rs.at[frm], (frm, s))

    def glast_copy(i):
        to = lax.rem(s + i, n_sub)
        return remote(gal_last, gal_full.at[gal_piece(s)], glast_ss.at[to], glast_rs.at[s], (g, to))

    def glast_from(i):
        frm = lax.rem(s + i, n_sub)
        return remote(gal_last, gal_full.at[gal_piece(frm)], glast_ss.at[frm], glast_rs.at[frm], (g, frm))

    @pl.loop(1, chips)
    def _(i):
        gal_from(i).wait_recv()
        gal_sum[...] += gal_recv[lax.rem(chip + i, chips)]

    @pl.loop(1, n_grp)
    def _(i):
        gsum_copy(i).start()

    @pl.loop(1, chips)
    def _(i):
        rhs_from(i).wait_recv()
        sum_send[:coarse, :] += rhs_recv[lax.rem(chip + i, chips)].astype(F32)

    @pl.loop(1, n_grp)
    def _(i):
        sum_copy(i).start()

    @pl.loop(late, chunks)
    def _(c):
        finish(c)

    gal_last[...] = gal_sum[...]

    @pl.loop(1, n_grp)
    def _(i):
        gsum_from(i).wait_recv()
        gal_last[...] += gal_sum_recv[lax.rem(g + i, n_grp)]

    gal_last[...] = gal_last[...] * scaling

    @pl.loop(1, n_sub)
    def _(i):
        glast_copy(i).start()

    sum_last[...] = sum_send[sum_piece(g), :]

    @pl.loop(1, n_grp)
    def _(i):
        sum_from(i).wait_recv()
        sum_last[...] += sum_recv[lax.rem(g + i, n_grp)]

    sum_last[...] = sum_last[...] * scaling

    @pl.loop(1, n_grp)
    def _(i):
        last_copy(i).start()

    gal_full[gal_piece(s), :] = gal_last[...]
    sum_full[sum_piece(g), :] = sum_last[...]

    @pl.loop(1, n_sub)
    def _(i):
        glast_from(i).wait_recv()

    gal_ref[...] = gal_full[:coarse, :]

    @pl.loop(1, n_grp)
    def _(i):
        last_from(i).wait_recv()

    rhs_ref[...] = sum_full[:coarse, :]

    for f in range(4):
        @pl.when(sends[f])
        def _():
            ext_copy(f).wait_send()

            @pl.loop(0, chunks)
            def _(c):
                face_copy(c, f).wait_send()

    @pl.loop(0, chunks)
    def _(c):
        when_relaying(c, lambda copy: copy.wait_send())

    gal_swap.wait_send()

    @pl.loop(0, chips)
    def _(i):
        pair_copy(i).wait_send()

    @pl.loop(1, chips)
    def _(i):
        rhs_copy(i).wait_send()
        gal_copy(i).wait_send()

    @pl.loop(1, n_sub)
    def _(i):
        glast_copy(i).wait_send()

    @pl.loop(1, n_grp)
    def _(i):
        gsum_copy(i).wait_send()
        sum_copy(i).wait_send()
        last_copy(i).wait_send()


def local(n_grp, n_sub, residual, inverse_blocks, operator_tiles, column_blocks, coarse_basis, face_rows):
    resid = residual[0, 0]
    inv = inverse_blocks[0, 0]
    tiles = operator_tiles[0, 0]
    basis = jnp.swapaxes(coarse_basis[0, 0], 0, 1)
    faces = face_rows[0, 0]
    rows, k = resid.shape
    coarse = basis.shape[0]
    ov = faces.shape[1]
    tile = tiles.shape[-1]
    ext_blocks = inv.shape[1] // tile
    part = k // n_sub
    width = max(512, part)
    chunks = k // width
    gal_rows = -(-coarse // (8 * n_sub)) * 8
    sum_rows = -(-coarse // (8 * n_grp)) * 8
    chips = n_sub // 2
    scaling = 1.0 / math.sqrt(rows * n_grp * n_sub)
    dma = pltpu.SemaphoreType.DMA
    hbm = pl.BlockSpec(memory_space=pl.ANY)
    vmem = pl.BlockSpec(memory_space=pltpu.VMEM)
    fix, gal, rhs = pl.pallas_call(
        functools.partial(kernel, n_grp, n_sub, width, scaling),
        out_shape=(
            pltpu.VMEM((rows, k), BF16),
            pltpu.VMEM((coarse, coarse), F32),
            pltpu.VMEM((coarse, part), F32),
        ),
        in_specs=[pl.BlockSpec(memory_space=pltpu.SMEM), vmem, vmem, hbm, hbm, hbm],
        out_specs=(vmem, vmem, vmem),
        scratch_shapes=[
            pltpu.VMEM((chunks, rows, width), BF16),
            pltpu.VMEM(inv.shape, BF16),
            pltpu.VMEM(tiles.shape, BF16),
            pltpu.VMEM((4 * ov, rows), BF16),
            pltpu.VMEM((4, coarse, tile), BF16),
            pltpu.VMEM((ext_blocks, coarse, tile), BF16),
            pltpu.VMEM((chunks, 4 * ov, width), BF16),
            pltpu.VMEM((chunks, 4 * ov, width), BF16),
            pltpu.VMEM((chunks, ov, width), BF16),
            pltpu.VMEM((chunks, rows, width), F32),
            pltpu.VMEM((chips, coarse, part), F32),
            pltpu.VMEM((chips, coarse, part), F32),
            pltpu.VMEM((chips, coarse, part), F32),
            pltpu.VMEM((chips, coarse, part), BF16),
            pltpu.VMEM((chips, coarse, part), BF16),
            pltpu.VMEM((n_grp * sum_rows, part), F32),
            pltpu.VMEM((n_grp, sum_rows, part), F32),
            pltpu.VMEM((sum_rows, part), F32),
            pltpu.VMEM((n_grp * sum_rows, part), F32),
            pltpu.VMEM((rows, coarse), BF16),
            pltpu.VMEM((n_sub * gal_rows, coarse), F32),
            pltpu.VMEM((n_sub * gal_rows, coarse), F32),
            pltpu.VMEM((n_sub * gal_rows, coarse), F32),
            pltpu.VMEM((chips, gal_rows, coarse), F32),
            pltpu.VMEM((gal_rows, coarse), F32),
            pltpu.VMEM((n_grp, gal_rows, coarse), F32),
            pltpu.VMEM((gal_rows, coarse), F32),
            pltpu.VMEM((n_sub * gal_rows, coarse), F32),
            dma((2,)),
            dma((chunks,)),
            dma((4,)),
            dma((4,)),
            dma((chunks, 4)),
            dma((chunks, 4)),
            dma((chunks,)),
            dma((chunks,)),
            dma((chips,)),
            dma((chips,)),
            dma((1,)),
            dma((1,)),
            dma((chips,)),
            dma((chips,)),
            dma((n_grp,)),
            dma((n_grp,)),
            dma((n_grp,)),
            dma((n_grp,)),
            dma((chips,)),
            dma((chips,)),
            dma((n_grp,)),
            dma((n_grp,)),
            dma((n_sub,)),
            dma((n_sub,)),
        ],
        compiler_params=pltpu.CompilerParams(
            collective_id=0, has_side_effects=True, vmem_limit_bytes=55 * 1024 * 1024
        ),
    )(column_blocks[0, 0], faces, basis, resid, inv, tiles)
    return fix[None, None], gal, rhs


def solution(mesh):
    return jax.shard_map(
        functools.partial(local, mesh.shape["grp"], mesh.shape["sub"]),
        mesh=mesh,
        in_specs=(
            P("grp", "sub", None, None),
            P("grp", "sub", None, None),
            P("grp", "sub", None, None, None, None),
            P("grp", "sub", None, None),
            P("grp", "sub", None, None),
            P("grp", "sub", None, None),
        ),
        out_specs=(P("grp", "sub", None, None), P(), P(None, "sub")),
        check_vma=False,
    )
```
